32 devices in a mesh: grp: 2 (over y), win: 4 (over z), uly: 4 (over x, core).
Axes of the slice: x: 2, y: 2, z: 4, core: 2. Of those that a mesh axis runs over, the one named last changes fastest.
Arguments:
- query_rows: bfloat16 [8, 16, 64, 5120], P(('grp', 'win'), None, 'uly'), parts along dimension 0, may hold values from -140 to 140
- key_rows: bfloat16 [8, 16, 64, 5120], P(('grp', 'win'), None, 'uly'), parts along dimension 0, may hold values from -140 to 140
- value_rows: bfloat16 [8, 16, 64, 5120], P(('grp', 'win'), None, 'uly'), parts along dimension 0, may hold values from -6 to 6
- query_gain: float32 [5120], replicated, may hold values from 0.25 to 1.75
- key_gain: float32 [5120], replicated, may hold values from 0.25 to 1.75
- window_start: int32 [8], P('grp'), parts along dimension 0, may hold values from 0 to 40, as said below
- owner_of_phase: int32 [8], P('grp'), parts along dimension 0, may hold values from 0 to 3, each once
- blend_weight: int32 [8, 16], P('grp'), parts along dimension 0, may hold values from 1 to 8
Outputs:
- owned_frames: bfloat16 [96, 64, 5120], P(('grp', 'win'), 'uly'), parts along dimension 0
- next_windows: bfloat16 [8, 16, 64, 5120], P(('grp', 'win'), None, 'uly'), parts along dimension 0
The draws below stay inside these ranges and needn't reach their ends.
There are 2 independent parts, one for each index of `grp`. The reference program is written for one: setup_inputs(seed, part) draws one part's arguments, and reference() takes and returns one part's arrays. A program takes and returns all parts, laid end to end along the dimension named above; an argument that names none is the same for every part. Nothing has to cross between parts.
Inputs may be any that keep to these rules, and one draw needn't show every extreme that they name: `window_start`: window w starts at frame w * 12 plus an offset of 0 to 4; in some pair of consecutive windows (the last one followed by the first counts as consecutive) the first offset is 4 and the second 0. `owner_of_phase`: a permutation.
All inputs are finite; a program needn't handle non-finite values.
Results may differ from the reference program's by a relative error of at most 0.0015.
The reference program's roundings to bfloat16 on the way count: a program that leaves them out, or rounds other values in their place, can miss the bound.
Values may be sent and summed in bfloat16 or wider, within the bound.
A program may use at most 128 MiB of HBM per device.

```python
import math
import jax
import jax.numpy as jnp
from jax import lax

D = 5120
HEADS = 40
HD = 128
P_SIZE = 64
WF = 16
FR = 12
SHIFT = 6
NW = 4
FRAMES = 48


def shared_layout(key):
    column_scale = jnp.exp(jax.random.uniform(jax.random.fold_in(key, 11), (D,), jnp.float32) * math.log(10.0))
    return column_scale


def draw_query_rows(key, part):
    column_scale = shared_layout(key)
    own_key = jax.random.fold_in(key, 21)
    drawn = jnp.clip(jax.random.normal(own_key, (NW, WF, P_SIZE, D), jnp.float32), -6.0, 6.0) * column_scale
    return drawn.astype(jnp.bfloat16)


def draw_key_rows(key, part):
    column_scale = shared_layout(key)
    own_key = jax.random.fold_in(key, 31)
    drawn = jnp.clip(jax.random.normal(own_key, (NW, WF, P_SIZE, D), jnp.float32), -6.0, 6.0) * column_scale
    return drawn.astype(jnp.bfloat16)


def draw_window_start(key, part):
    offsets = jax.random.randint(jax.random.fold_in(key, 41), (NW,), 0, WF - FR + 1)
    chosen = jax.random.randint(jax.random.fold_in(key, 42), (), 0, NW)
    window_index = jnp.arange(NW)
    offsets = jnp.where(window_index == chosen, WF - FR, offsets)
    offsets = jnp.where(window_index == (chosen + 1) % NW, 0, offsets)
    return (window_index * FR + offsets).astype(jnp.int32)


def plant(entries, rng, least, high):
    extent = entries.shape
    place = [jax.random.randint(jax.random.fold_in(rng, axis), (), 0, extent[axis]) for axis in range(len(extent))]
    entries = entries.at[tuple(place)].set(least)
    longest = extent.index(max(extent))
    place[longest] = (place[longest] + 1) % extent[longest]
    return entries.at[tuple(place)].set(high)


def levels(rng, extent, shards, least, largest):
    def one(dim, parts):
        draws = jax.random.uniform(jax.random.fold_in(jax.random.fold_in(rng, 6), dim), (parts,), jnp.float32, least / len(shards), largest / len(shards))
        return jnp.repeat(jnp.exp(draws), extent[dim] // parts).reshape((-1,) + (1,) * (len(extent) - dim - 1))

    loudness = one(*shards[0])
    for cut in shards[1:]:
        loudness = loudness * one(*cut)
    return loudness


def noise(stream_key, shape, scale, reach, pieces=(), held_as=jnp.bfloat16):
    entries = scale * jax.random.normal(stream_key, shape, jnp.float32)
    if pieces:
        entries = entries * levels(stream_key, shape, pieces, -0.22, 0.18)
    return jnp.clip(entries, -reach, reach).astype(held_as)


def setup_inputs(seed: int = 0, part: int = 0) -> dict:
    key_list = jax.random.split(jax.random.key(seed), 9)
    own_keys = jax.random.split(jax.random.fold_in(key_list[8], part), 9)
    query_rows = draw_query_rows(jax.random.fold_in(jax.random.fold_in(key_list[8], part), 71), part)
    key_rows = draw_key_rows(jax.random.fold_in(jax.random.fold_in(key_list[8], part), 71), part)
    value_rows = noise(own_keys[2], (NW, WF, P_SIZE, D), 1.0, 6.0, ((0, 4), (2, 4)))
    query_gain = jnp.clip(1.0 + 0.15 * jax.random.normal(key_list[3], (D,), jnp.float32), 0.25, 1.75)
    key_gain = jnp.clip(1.0 + 0.15 * jax.random.normal(key_list[4], (D,), jnp.float32), 0.25, 1.75)
    window_start = draw_window_start(jax.random.fold_in(jax.random.fold_in(key_list[8], part), 71), part)
    owner_of_phase = jax.random.permutation(own_keys[6], NW).astype(jnp.int32)
    blend_weight = plant(jax.random.randint(own_keys[7], (NW, WF), 1, 9), jax.random.fold_in(own_keys[7], 1), 1, 8).astype(jnp.int32)
    return dict(query_rows=query_rows, key_rows=key_rows, value_rows=value_rows, query_gain=query_gain, key_gain=key_gain, window_start=window_start, owner_of_phase=owner_of_phase, blend_weight=blend_weight)


def normalize(row_block, gain_vector):
    floats = row_block.astype(jnp.float32)
    mean_square = lax.optimization_barrier(jnp.mean(floats * floats, axis=-1, keepdims=True))
    return (floats * lax.rsqrt(mean_square + 1e-06) * gain_vector).astype(jnp.bfloat16)

def head_attention(operands):
    query_head, key_head, value_head = operands
    scores = jnp.dot(query_head, key_head.T, preferred_element_type=jnp.float32) * (1.0 / math.sqrt(query_head.shape[-1]))
    row_max = lax.optimization_barrier(jnp.max(scores, axis=-1, keepdims=True))
    exponent = jnp.exp(scores - row_max)
    weights = (exponent / lax.optimization_barrier(jnp.sum(exponent, axis=-1, keepdims=True))).astype(jnp.bfloat16)
    return jnp.dot(weights, value_head, preferred_element_type=jnp.float32).astype(jnp.bfloat16)

def reference(query_rows, key_rows, value_rows, query_gain, key_gain, window_start, owner_of_phase, blend_weight):
    token_count = WF * P_SIZE

    def split_heads(tensor):
        return jnp.moveaxis(tensor.reshape(token_count, HEADS, HD), 1, 0)

    def window_attention(operands):
        query_win, key_win, value_win = operands
        result = lax.map(head_attention, (split_heads(normalize(query_win, query_gain)), split_heads(normalize(key_win, key_gain)), split_heads(value_win)))
        return jnp.moveaxis(result, 0, 1).reshape(WF, P_SIZE, D)
    window_out = lax.map(window_attention, (query_rows, key_rows, value_rows))
    frame_range = jnp.arange(WF, dtype=jnp.int32)
    frame_of = ((window_start[:, None] + frame_range[None, :]) % FRAMES).reshape(-1).astype(jnp.int32)
    weight_float = blend_weight.astype(jnp.float32)
    terms = (weight_float[:, :, None, None] * window_out.astype(jnp.float32)).reshape(NW * WF, P_SIZE, D)
    numerator = jnp.zeros((FRAMES, P_SIZE, D), jnp.float32).at[frame_of].add(terms)
    denominator = jnp.zeros((FRAMES,), jnp.float32).at[frame_of].add(weight_float.reshape(-1))
    blended = (numerator / denominator[:, None, None]).astype(jnp.bfloat16)
    phase_range = jnp.arange(NW, dtype=jnp.int32)
    inverse = jnp.zeros((NW,), jnp.int32).at[owner_of_phase].set(phase_range)
    owned_index = (jnp.arange(FR, dtype=jnp.int32)[None, :] * NW + inverse[:, None]).reshape(-1).astype(jnp.int32)
    owned_frames = blended[owned_index]
    next_index = ((window_start[:, None] + SHIFT + frame_range[None, :]) % FRAMES).reshape(-1).astype(jnp.int32)
    next_windows = blended[next_index].reshape(NW, WF, P_SIZE, D)
    return (owned_frames, next_windows)
```

```python
import functools
import math

import jax
import jax.numpy as jnp
from jax import lax
from jax.experimental import pallas as pl
from jax.experimental.pallas import tpu as pltpu
from jax.sharding import PartitionSpec as P

HEADS = 40
WF = 16
FR = 12
AHEAD = 2
LAG_BLEND = 1
LAG_RETURN = 2
LAG_LAST = 3
ROWS = 16


def fused(
    dims,
    send_pos,
    first_at,
    second_at,
    first_w,
    second_w,
    total_w,
    target_slot,
    next_at,
    q_ref,
    k_ref,
    v_ref,
    qg_ref,
    kg_ref,
    owned_ref,
    next_ref,
    stage,
    inbox,
    vbox,
    attended,
    z_out,
    z_in,
    x_out,
    x_in,
    r_out,
    r_in,
    z_now,
    x_now,
    qk_send,
    qk_recv,
    v_send,
    v_recv,
    zo_send,
    zo_recv,
    xo_send,
    xo_recv,
    ro_send,
    ro_recv,
):
    ulysses, windows, capacity, steps, head, tokens = dims
    local = tokens // WF
    me = lax.axis_index("uly")
    my_window = lax.axis_index("win")

    def peer(d):
        return lax.rem(me + d, ulysses)

    def far(d):
        return lax.rem(my_window + d, windows)

    barrier = pltpu.get_barrier_semaphore()
    for d in range(1, ulysses):
        pl.semaphore_signal(
            barrier, inc=1, device_id={"uly": peer(d)}, device_id_type=pl.DeviceIdType.MESH
        )
    for d in range(1, windows):
        pl.semaphore_signal(
            barrier, inc=1, device_id={"win": far(d)}, device_id_type=pl.DeviceIdType.MESH
        )
    pl.semaphore_wait(barrier, ulysses + windows - 2)

    def spread(source, target, send, recv, axis):
        mine = me if axis == "uly" else my_window
        count = ulysses if axis == "uly" else windows
        for d in range(1, count):
            to = lax.rem(mine + d, count)
            pltpu.make_async_remote_copy(
                src_ref=source(to),
                dst_ref=target(mine),
                send_sem=send,
                recv_sem=recv,
                device_id={axis: to},
                device_id_type=pl.DeviceIdType.MESH,
            ).start()
        pltpu.make_async_copy(source(mine), target(mine), recv).start()

    def arrived(ref, sem):
        pltpu.make_async_copy(ref, ref, sem).wait()

    def columns(u, s):
        return pl.ds(pl.multiple_of((u * steps + s) * head, head), head)

    def send_values(s):
        spread(
            lambda u: v_ref.at[:, columns(u, s)],
            lambda u: vbox.at[s, u],
            v_send.at[s],
            v_recv.at[s],
            "uly",
        )

    def send_scored(s):
        spread(
            lambda u: stage.at[u, s],
            lambda u: inbox.at[s, u],
            qk_send.at[s],
            qk_recv.at[s],
            "uly",
        )

    for s in range(AHEAD):
        send_values(s)

    def norm_block(t, carry):
        rows = pl.ds(pl.multiple_of(t * ROWS, ROWS), ROWS)
        for which, (ref, gain) in enumerate(((q_ref, qg_ref), (k_ref, kg_ref))):
            floats = ref[rows, :].astype(jnp.float32)
            mean_square = jnp.mean(floats * floats, axis=-1, keepdims=True)
            scaled = (floats * lax.rsqrt(mean_square + 1e-06) * gain[...]).astype(jnp.bfloat16)
            for u in range(ulysses):
                for s in range(steps):
                    at = (u * steps + s) * head
                    stage[u, s, which, rows, :] = scaled[:, at : at + head]
        return carry

    lax.fori_loop(0, tokens // ROWS, norm_block, 0)
    for s in range(AHEAD):
        send_scored(s)

    scale = 1.0 / math.sqrt(head)

    def attention(s):
        arrived(inbox.at[s], qk_recv.at[s])
        arrived(vbox.at[s], v_recv.at[s])

        @pl.when(s + AHEAD < steps)
        def _():
            send_scored(s + AHEAD)
            send_values(s + AHEAD)

        keys = inbox[s, :, 1].reshape(ulysses * tokens, head)
        values = vbox[s].reshape(ulysses * tokens, head)
        for u in range(ulysses):
            scores = (
                lax.dot_general(
                    inbox[s, u, 0],
                    keys,
                    (((1,), (1,)), ((), ())),
                    preferred_element_type=jnp.float32,
                )
                * scale
            )
            exponent = jnp.exp(scores - jnp.max(scores, axis=-1, keepdims=True))
            inverse_sum = 1.0 / jnp.sum(exponent, axis=-1, keepdims=True)
            weights = (exponent * inverse_sum).astype(jnp.bfloat16)
            result = jnp.dot(weights, values, preferred_element_type=jnp.float32)
            attended[:, u] = result.astype(jnp.bfloat16).reshape(WF, local, head)
        for o in range(windows):
            for c in range(capacity):
                z_out[s, o, c] = attended[send_pos[o * capacity + c]]
        spread(
            lambda o: z_out.at[s, o],
            lambda o: z_in.at[s, pl.ds(o * capacity, capacity)],
            zo_send.at[s],
            zo_recv.at[s],
            "win",
        )

    def blend(s):
        arrived(z_in.at[s], zo_recv.at[s])
        z_now[...] = z_in[s]
        for f in range(FR):
            numerator = first_w[f] * z_now[first_at[f]].astype(jnp.float32)
            numerator += second_w[f] * z_now[second_at[f]].astype(jnp.float32)
            x_out[s, :, f] = (numerator / total_w[f]).astype(jnp.bfloat16)
        spread(
            lambda u: x_out.at[s, u],
            lambda u: x_in.at[s, u],
            xo_send.at[s],
            xo_recv.at[s],
            "uly",
        )

    def give_back(s):
        arrived(x_in.at[s], xo_recv.at[s])
        x_now[...] = x_in[s]
        for o in range(windows):
            for c in range(capacity):
                r_out[s, o, c] = x_now[:, target_slot[o * capacity + c]]
        spread(
            lambda o: r_out.at[s, o],
            lambda o: r_in.at[s, pl.ds(o * capacity, capacity)],
            ro_send.at[s],
            ro_recv.at[s],
            "win",
        )
        for u in range(ulysses):
            owned_ref[:, :, columns(u, s)] = x_in[s, u]

    def finish(s):
        arrived(r_in.at[s], ro_recv.at[s])
        z_now[...] = r_in[s]
        for j in range(WF):
            frame = z_now[next_at[j]]
            for u in range(ulysses):
                next_ref[j, :, columns(u, s)] = frame[u]

    def step(i, carry):
        for lag, work in (
            (0, attention),
            (LAG_BLEND, blend),
            (LAG_RETURN, give_back),
            (LAG_LAST, finish),
        ):

            @pl.when((i >= lag) & (i < steps + lag))
            def _(lag=lag, work=work):
                work(i - lag)

        return carry

    lax.fori_loop(0, steps + LAG_LAST, step, 0)

    def sent(s, carry):
        arrived(inbox.at[s, pl.ds(0, ulysses - 1)], qk_send.at[s])
        arrived(vbox.at[s, pl.ds(0, ulysses - 1)], v_send.at[s])
        arrived(z_out.at[s, pl.ds(0, windows - 1)], zo_send.at[s])
        arrived(x_out.at[s, pl.ds(0, ulysses - 1)], xo_send.at[s])
        arrived(r_out.at[s, pl.ds(0, windows - 1)], ro_send.at[s])
        return carry

    lax.fori_loop(0, steps, sent, 0)


def per_device(
    query_rows,
    key_rows,
    value_rows,
    query_gain,
    key_gain,
    window_start,
    owner_of_phase,
    blend_weight,
):
    windows = lax.axis_size("win")
    ulysses = lax.axis_size("uly")
    position = lax.axis_index("win")
    frames_total = FR * windows
    capacity = (WF + windows - 1) // windows
    shift_frames = FR // 2
    local = query_rows.shape[2]
    features = query_rows.shape[3]
    head = features // HEADS
    steps = HEADS // ulysses
    tokens = WF * local

    phases = jnp.arange(windows, dtype=jnp.int32)
    inverse = jnp.sum(
        jnp.where(owner_of_phase[None, :] == phases[:, None], phases[None, :], 0), axis=1
    )
    my_start = window_start[position]
    my_phase = inverse[position]
    slots = jnp.arange(capacity, dtype=jnp.int32)
    send_pos = (inverse[:, None] - my_start) % windows + slots[None, :] * windows
    send_pos = jnp.minimum(send_pos, WF - 1).reshape(-1)

    frames = jnp.arange(FR, dtype=jnp.int32) * windows + my_phase
    offset = (frames[None, :] - window_start[:, None]) % frames_total
    holds = offset < WF
    factor = jnp.sum(
        jnp.where(
            offset[..., None] == jnp.arange(WF, dtype=jnp.int32), blend_weight[:, None, :], 0
        ),
        axis=-1,
    ).astype(jnp.float32)
    place = phases[:, None] * capacity + offset // windows
    first_window = jnp.min(jnp.where(holds, phases[:, None], windows), axis=0)
    last_window = jnp.max(jnp.where(holds, phases[:, None], -1), axis=0)
    is_first = phases[:, None] == first_window[None, :]
    is_last = phases[:, None] == last_window[None, :]
    is_other = is_last & ~is_first
    first_at = jnp.sum(jnp.where(is_first, place, 0), axis=0)
    second_at = jnp.sum(jnp.where(is_last, place, 0), axis=0)
    first_w = jnp.sum(jnp.where(is_first, factor, 0), axis=0)
    second_w = jnp.sum(jnp.where(is_other, factor, 0), axis=0)
    total_w = first_w + second_w

    target_pos = (my_phase - window_start[:, None] - shift_frames) % windows + slots[
        None, :
    ] * windows
    target_slot = (
        (window_start[:, None] + shift_frames + target_pos) % frames_total // windows
    ).reshape(-1)
    order = jnp.arange(WF, dtype=jnp.int32)
    needed = (my_start + shift_frames + order) % windows
    source = jnp.sum(jnp.where(needed[:, None] == phases[None, :], owner_of_phase[None, :], 0), 1)
    next_at = source * capacity + order // windows

    smem = pl.BlockSpec(memory_space=pltpu.SMEM)
    vmem = pl.BlockSpec(memory_space=pltpu.VMEM)
    bf16 = jnp.bfloat16
    sems = pltpu.SemaphoreType.DMA((steps,))
    frame = (ulysses, local, head)
    owned, next_rows = pl.pallas_call(
        functools.partial(fused, (ulysses, windows, capacity, steps, head, tokens)),
        out_shape=(
            jax.ShapeDtypeStruct((FR, local, features), bf16),
            jax.ShapeDtypeStruct((WF, local, features), bf16),
        ),
        in_specs=[smem] * 8 + [vmem] * 5,
        out_specs=(vmem, vmem),
        scratch_shapes=[
            pltpu.VMEM((ulysses, steps, 2, tokens, head), bf16),
            pltpu.VMEM((steps, ulysses, 2, tokens, head), bf16),
            pltpu.VMEM((steps, ulysses, tokens, head), bf16),
            pltpu.VMEM((WF,) + frame, bf16),
            pltpu.VMEM((steps, windows, capacity) + frame, bf16),
            pltpu.VMEM((steps, windows * capacity) + frame, bf16),
            pltpu.VMEM((steps, ulysses, FR, local, head), bf16),
            pltpu.VMEM((steps, ulysses, FR, local, head), bf16),
            pltpu.VMEM((steps, windows, capacity) + frame, bf16),
            pltpu.VMEM((steps, windows * capacity) + frame, bf16),
            pltpu.VMEM((windows * capacity,) + frame, bf16),
            pltpu.VMEM((ulysses, FR, local, head), bf16),
        ]
        + [sems] * 10,
        compiler_params=pltpu.CompilerParams(
            collective_id=0, has_side_effects=True, vmem_limit_bytes=66 * 1000 * 1000
        ),
    )(
        send_pos,
        first_at,
        second_at,
        first_w,
        second_w,
        total_w,
        target_slot,
        next_at,
        query_rows.reshape(tokens, features),
        key_rows.reshape(tokens, features),
        value_rows.reshape(tokens, features),
        query_gain.reshape(1, features),
        key_gain.reshape(1, features),
    )
    return (owned, next_rows[None])


def solution(mesh):
    placed = (
        P(("grp", "win"), None, "uly", None),
        P(("grp", "win"), None, "uly", None),
        P(("grp", "win"), None, "uly", None),
        P(),
        P(),
        P("grp"),
        P("grp"),
        P("grp", None),
    )
    return jax.shard_map(
        per_device,
        mesh=mesh,
        in_specs=placed,
        out_specs=(P(("grp", "win"), "uly", None), P(("grp", "win"), None, "uly", None)),
        check_vma=False,
    )
```

```python
import functools
import math

import jax
import jax.numpy as jnp
from jax import lax
from jax.experimental import pallas as pl
from jax.experimental.pallas import tpu as pltpu
from jax.sharding import PartitionSpec as P

HEADS = 40
WF = 16
FR = 12
AHEAD = 2
LAG_BLEND = 1
LAG_RETURN = 2
LAG_LAST = 3
ROWS = 16


def fused(
    dims,
    start_ref,
    owner_ref,
    weight_ref,
    q_ref,
    k_ref,
    v_ref,
    qg_ref,
    kg_ref,
    owned_ref,
    next_ref,
    stage,
    inbox,
    vbox,
    attended,
    z_out,
    z_in,
    x_out,
    x_in,
    r_out,
    r_in,
    z_now,
    x_now,
    inverse,
    send_pos,
    first_at,
    second_at,
    first_w,
    second_w,
    target_slot,
    next_at,
    q_send,
    q_recv,
    k_send,
    k_recv,
    v_send,
    v_recv,
    zo_send,
    zo_recv,
    xo_send,
    xo_recv,
    ro_send,
    ro_recv,
):
    ulysses, windows, capacity, steps, head, tokens = dims
    local = tokens // WF
    me = lax.axis_index("uly")
    my_window = lax.axis_index("win")

    def peer(d):
        return lax.rem(me + d, ulysses)

    def far(d):
        return lax.rem(my_window + d, windows)

    barrier = pltpu.get_barrier_semaphore()
    for d in range(1, ulysses):
        pl.semaphore_signal(
            barrier, inc=1, device_id={"uly": peer(d)}, device_id_type=pl.DeviceIdType.MESH
        )
    for d in range(1, windows):
        pl.semaphore_signal(
            barrier, inc=1, device_id={"win": far(d)}, device_id_type=pl.DeviceIdType.MESH
        )
    pl.semaphore_wait(barrier, ulysses + windows - 2)

    def spread(source, target, send, recv, axis):
        mine = me if axis == "uly" else my_window
        count = ulysses if axis == "uly" else windows
        for d in range(1, count):
            to = lax.rem(mine + d, count)
            pltpu.make_async_remote_copy(
                src_ref=source(to),
                dst_ref=target(mine),
                send_sem=send,
                recv_sem=recv,
                device_id={axis: to},
                device_id_type=pl.DeviceIdType.MESH,
            ).start()
        pltpu.make_async_copy(source(mine), target(mine), recv).start()

    def arrived(ref, sem):
        pltpu.make_async_copy(ref, ref, sem).wait()

    def columns(u, s):
        return pl.ds(pl.multiple_of((u * steps + s) * head, head), head)

    def send_values(s):
        spread(
            lambda u: v_ref.at[:, columns(u, s)],
            lambda u: vbox.at[s, u],
            v_send.at[s],
            v_recv.at[s],
            "uly",
        )

    def send_scored(which, s):
        spread(
            lambda u: stage.at[which, u, s],
            lambda u: inbox.at[which, s, u],
            (q_send, k_send)[which].at[s],
            (q_recv, k_recv)[which].at[s],
            "uly",
        )

    for s in range(AHEAD):
        send_values(s)

    frames_total = FR * windows
    shift = FR // 2

    def tables():
        my_start = start_ref[my_window]

        def invert(o, carry):
            def seek(phase, found):
                return jnp.where(owner_ref[phase] == o, phase, found)

            inverse[o] = lax.fori_loop(0, windows, seek, jnp.int32(0))
            return carry

        lax.fori_loop(0, windows, invert, 0)
        my_phase = inverse[my_window]

        def per_window(o, carry):
            for c in range(capacity):
                ahead = lax.rem(inverse[o] - my_start + frames_total, windows) + c * windows
                send_pos[o * capacity + c] = jnp.minimum(ahead, WF - 1)
                base = start_ref[o] + shift
                wanted = lax.rem(my_phase - base + 2 * frames_total, windows) + c * windows
                target_slot[o * capacity + c] = lax.rem(base + wanted, frames_total) // windows
            return carry

        lax.fori_loop(0, windows, per_window, 0)

        for f in range(FR):
            frame = f * windows + my_phase
            home = frame // FR
            before = lax.rem(home + windows - 1, windows)
            weight, place = [], []
            for w in (home, before):
                offset = lax.rem(frame - start_ref[w] + frames_total, frames_total)
                held = jnp.minimum(offset, WF - 1)
                weight.append(jnp.where(offset < WF, weight_ref[w, held], 0).astype(jnp.float32))
                place.append(w * capacity + held // windows)
            first_w[f], second_w[f] = weight
            first_at[f], second_at[f] = place
        for j in range(WF):
            needed = lax.rem(my_start + shift + j, windows)
            next_at[j] = owner_ref[needed] * capacity + j // windows

    for which, (ref, gain) in enumerate(((q_ref, qg_ref), (k_ref, kg_ref))):

        def norm_block(t, carry, which=which, ref=ref, gain=gain):
            rows = pl.ds(pl.multiple_of(t * ROWS, ROWS), ROWS)
            floats = ref[rows, :].astype(jnp.float32)
            mean_square = jnp.mean(floats * floats, axis=-1, keepdims=True)
            scaled = (floats * lax.rsqrt(mean_square + 1e-06) * gain[...]).astype(jnp.bfloat16)
            for u in range(ulysses):
                for s in range(steps):
                    at = (u * steps + s) * head
                    stage[which, u, s, rows, :] = scaled[:, at : at + head]
            return carry

        lax.fori_loop(0, tokens // ROWS, norm_block, 0)
        for s in range(AHEAD):
            send_scored(which, s)

    tables()

    scale = 1.0 / math.sqrt(head)

    def attention(s):
        arrived(inbox.at[0, s], q_recv.at[s])
        arrived(inbox.at[1, s], k_recv.at[s])
        arrived(vbox.at[s], v_recv.at[s])

        @pl.when(s + AHEAD < steps)
        def _():
            send_scored(0, s + AHEAD)
            send_scored(1, s + AHEAD)
            send_values(s + AHEAD)

        keys = inbox[1, s].reshape(ulysses * tokens, head)
        values = vbox[s].reshape(ulysses * tokens, head)
        for u in range(ulysses):
            scores = (
                lax.dot_general(
                    inbox[0, s, u],
                    keys,
                    (((1,), (1,)), ((), ())),
                    preferred_element_type=jnp.float32,
                )
                * scale
            )
            exponent = jnp.exp(scores - jnp.max(scores, axis=-1, keepdims=True))
            inverse_sum = 1.0 / jnp.sum(exponent, axis=-1, keepdims=True)
            weights = (exponent * inverse_sum).astype(jnp.bfloat16)
            result = jnp.dot(weights, values, preferred_element_type=jnp.float32)
            attended[:, u] = result.astype(jnp.bfloat16).reshape(WF, local, head)
        for o in range(windows):
            for c in range(capacity):
                z_out[s, o, c] = attended[send_pos[o * capacity + c]]
        spread(
            lambda o: z_out.at[s, o],
            lambda o: z_in.at[s, pl.ds(o * capacity, capacity)],
            zo_send.at[s],
            zo_recv.at[s],
            "win",
        )

    def blend(s):
        arrived(z_in.at[s], zo_recv.at[s])
        z_now[...] = z_in[s]
        for f in range(FR):
            numerator = first_w[f] * z_now[first_at[f]].astype(jnp.float32)
            numerator += second_w[f] * z_now[second_at[f]].astype(jnp.float32)
            x_out[s, :, f] = (numerator / (first_w[f] + second_w[f])).astype(jnp.bfloat16)
        spread(
            lambda u: x_out.at[s, u],
            lambda u: x_in.at[s, u],
            xo_send.at[s],
            xo_recv.at[s],
            "uly",
        )

    def give_back(s):
        arrived(x_in.at[s], xo_recv.at[s])
        x_now[...] = x_in[s]
        for o in range(windows):
            for c in range(capacity):
                r_out[s, o, c] = x_now[:, target_slot[o * capacity + c]]
        spread(
            lambda o: r_out.at[s, o],
            lambda o: r_in.at[s, pl.ds(o * capacity, capacity)],
            ro_send.at[s],
            ro_recv.at[s],
            "win",
        )
        for u in range(ulysses):
            owned_ref[:, :, columns(u, s)] = x_in[s, u]

    def finish(s):
        arrived(r_in.at[s], ro_recv.at[s])
        z_now[...] = r_in[s]
        for j in range(WF):
            frame = z_now[next_at[j]]
            for u in range(ulysses):
                next_ref[j, :, columns(u, s)] = frame[u]

    def step(i, carry):
        for lag, work in (
            (0, attention),
            (LAG_BLEND, blend),
            (LAG_RETURN, give_back),
            (LAG_LAST, finish),
        ):

            @pl.when((i >= lag) & (i < steps + lag))
            def _(lag=lag, work=work):
                work(i - lag)

        return carry

    lax.fori_loop(0, steps + LAG_LAST, step, 0)

    def sent(s, carry):
        arrived(inbox.at[0, s, pl.ds(0, ulysses - 1)], q_send.at[s])
        arrived(inbox.at[1, s, pl.ds(0, ulysses - 1)], k_send.at[s])
        arrived(vbox.at[s, pl.ds(0, ulysses - 1)], v_send.at[s])
        arrived(z_out.at[s, pl.ds(0, windows - 1)], zo_send.at[s])
        arrived(x_out.at[s, pl.ds(0, ulysses - 1)], xo_send.at[s])
        arrived(r_out.at[s, pl.ds(0, windows - 1)], ro_send.at[s])
        return carry

    lax.fori_loop(0, steps, sent, 0)


def per_device(
    query_rows,
    key_rows,
    value_rows,
    query_gain,
    key_gain,
    window_start,
    owner_of_phase,
    blend_weight,
):
    windows = lax.axis_size("win")
    ulysses = lax.axis_size("uly")
    capacity = (WF + windows - 1) // windows
    local = query_rows.shape[2]
    features = query_rows.shape[3]
    head = features // HEADS
    steps = HEADS // ulysses
    tokens = WF * local
    smem = pl.BlockSpec(memory_space=pltpu.SMEM)
    vmem = pl.BlockSpec(memory_space=pltpu.VMEM)
    bf16 = jnp.bfloat16
    sems = pltpu.SemaphoreType.DMA((steps,))
    frame = (ulysses, local, head)
    owned, next_rows = pl.pallas_call(
        functools.partial(fused, (ulysses, windows, capacity, steps, head, tokens)),
        out_shape=(
            jax.ShapeDtypeStruct((FR, local, features), bf16),
            jax.ShapeDtypeStruct((WF, local, features), bf16),
        ),
        in_specs=[smem] * 3 + [vmem] * 5,
        out_specs=(vmem, vmem),
        scratch_shapes=[
            pltpu.VMEM((2, ulysses, steps, tokens, head), bf16),
            pltpu.VMEM((2, steps, ulysses, tokens, head), bf16),
            pltpu.VMEM((steps, ulysses, tokens, head), bf16),
            pltpu.VMEM((WF,) + frame, bf16),
            pltpu.VMEM((steps, windows, capacity) + frame, bf16),
            pltpu.VMEM((steps, windows * capacity) + frame, bf16),
            pltpu.VMEM((steps, ulysses, FR, local, head), bf16),
            pltpu.VMEM((steps, ulysses, FR, local, head), bf16),
            pltpu.VMEM((steps, windows, capacity) + frame, bf16),
            pltpu.VMEM((steps, windows * capacity) + frame, bf16),
            pltpu.VMEM((windows * capacity,) + frame, bf16),
            pltpu.VMEM((ulysses, FR, local, head), bf16),
            pltpu.SMEM((windows,), jnp.int32),
            pltpu.SMEM((windows * capacity,), jnp.int32),
            pltpu.SMEM((FR,), jnp.int32),
            pltpu.SMEM((FR,), jnp.int32),
            pltpu.SMEM((FR,), jnp.float32),
            pltpu.SMEM((FR,), jnp.float32),
            pltpu.SMEM((windows * capacity,), jnp.int32),
            pltpu.SMEM((WF,), jnp.int32),
        ]
        + [sems] * 12,
        compiler_params=pltpu.CompilerParams(
            collective_id=0, has_side_effects=True, vmem_limit_bytes=66 * 1000 * 1000
        ),
    )(
        window_start,
        owner_of_phase,
        blend_weight,
        query_rows.reshape(tokens, features),
        key_rows.reshape(tokens, features),
        value_rows.reshape(tokens, features),
        query_gain.reshape(1, features),
        key_gain.reshape(1, features),
    )
    return (owned, next_rows[None])


def solution(mesh):
    placed = (
        P(("grp", "win"), None, "uly", None),
        P(("grp", "win"), None, "uly", None),
        P(("grp", "win"), None, "uly", None),
        P(),
        P(),
        P("grp"),
        P("grp"),
        P("grp", None),
    )
    return jax.shard_map(
        per_device,
        mesh=mesh,
        in_specs=placed,
        out_specs=(P(("grp", "win"), "uly", None), P(("grp", "win"), None, "uly", None)),
        check_vma=False,
    )
```

```python
import functools
import math

import jax
import jax.numpy as jnp
from jax import lax
from jax.experimental import pallas as pl
from jax.experimental.pallas import tpu as pltpu
from jax.sharding import PartitionSpec as P

HEADS = 40
WF = 16
FR = 12
AHEAD = 1
VALUES_AHEAD = 2
CHUNKS = 4
LAG_BLEND = 1
LAG_RETURN = 2
LAG_LAST = 3
ROWS = 16


def fused(
    dims,
    start_ref,
    owner_ref,
    weight_ref,
    q_ref,
    k_ref,
    v_ref,
    qg_ref,
    kg_ref,
    owned_ref,
    next_ref,
    q_now,
    k_now,
    next_out,
    stage,
    inbox,
    vbox,
    attended,
    z_out,
    z_in,
    x_out,
    x_in,
    r_out,
    r_in,
    z_now,
    x_now,
    inverse,
    send_pos,
    first_at,
    second_at,
    first_w,
    second_w,
    target_slot,
    next_at,
    q_send,
    q_recv,
    k_send,
    k_recv,
    v_send,
    v_recv,
    zo_send,
    zo_recv,
    xo_send,
    xo_recv,
    ro_send,
    ro_recv,
    own_sem,
    next_sem,
    q_load,
    k_load,
):
    ulysses, windows, capacity, steps, head, tokens = dims
    local = tokens // WF
    me = lax.axis_index("uly")
    my_window = lax.axis_index("win")

    def peer(d):
        return lax.rem(me + d, ulysses)

    def far(d):
        return lax.rem(my_window + d, windows)

    chunk = tokens // CHUNKS

    def load(ref, now, sem, c):
        rows = pl.ds(pl.multiple_of(c * chunk, chunk), chunk)
        return pltpu.make_async_copy(ref.at[rows], now.at[rows], sem.at[c])

    for ref, now, sem in ((q_ref, q_now, q_load), (k_ref, k_now, k_load)):
        for c in range(CHUNKS):
            load(ref, now, sem, c).start()

    barrier = pltpu.get_barrier_semaphore()
    for d in range(1, ulysses):
        pl.semaphore_signal(
            barrier, inc=1, device_id={"uly": peer(d)}, device_id_type=pl.DeviceIdType.MESH
        )
    for d in range(1, windows):
        pl.semaphore_signal(
            barrier, inc=1, device_id={"win": far(d)}, device_id_type=pl.DeviceIdType.MESH
        )
    pl.semaphore_wait(barrier, ulysses + windows - 2)

    def spread(source, target, send, recv, axis):
        mine = me if axis == "uly" else my_window
        count = ulysses if axis == "uly" else windows
        for d in range(1, count):
            to = lax.rem(mine + d, count)
            pltpu.make_async_remote_copy(
                src_ref=source(to),
                dst_ref=target(mine),
                send_sem=send,
                recv_sem=recv,
                device_id={axis: to},
                device_id_type=pl.DeviceIdType.MESH,
            ).start()
        pltpu.make_async_copy(source(mine), target(mine), recv).start()

    def arrived(ref, sem):
        pltpu.make_async_copy(ref, ref, sem).wait()

    def columns(u, s):
        return pl.ds(pl.multiple_of((u * steps + s) * head, head), head)

    def send_values(s):
        spread(
            lambda u: v_ref.at[:, columns(u, s)],
            lambda u: vbox.at[s, u],
            v_send.at[s],
            v_recv.at[s],
            "uly",
        )

    def send_scored(which, s):
        spread(
            lambda u: stage.at[which, u, s],
            lambda u: inbox.at[which, s, u],
            (q_send, k_send)[which].at[s],
            (q_recv, k_recv)[which].at[s],
            "uly",
        )

    for s in range(VALUES_AHEAD):
        send_values(s)

    frames_total = FR * windows
    shift = FR // 2

    def tables():
        my_start = start_ref[my_window]

        def invert(o, carry):
            def seek(phase, found):
                return jnp.where(owner_ref[phase] == o, phase, found)

            inverse[o] = lax.fori_loop(0, windows, seek, jnp.int32(0))
            return carry

        lax.fori_loop(0, windows, invert, 0)
        my_phase = inverse[my_window]

        def per_window(o, carry):
            for c in range(capacity):
                ahead = lax.rem(inverse[o] - my_start + frames_total, windows) + c * windows
                send_pos[o * capacity + c] = jnp.minimum(ahead, WF - 1)
                base = start_ref[o] + shift
                wanted = lax.rem(my_phase - base + 2 * frames_total, windows) + c * windows
                target_slot[o * capacity + c] = lax.rem(base + wanted, frames_total) // windows
            return carry

        lax.fori_loop(0, windows, per_window, 0)

        for f in range(FR):
            frame = f * windows + my_phase
            home = frame // FR
            before = lax.rem(home + windows - 1, windows)
            weight, place = [], []
            for w in (home, before):
                offset = lax.rem(frame - start_ref[w] + frames_total, frames_total)
                held = jnp.minimum(offset, WF - 1)
                weight.append(jnp.where(offset < WF, weight_ref[w, held], 0).astype(jnp.float32))
                place.append(w * capacity + held // windows)
            first_w[f], second_w[f] = weight
            first_at[f], second_at[f] = place
        for j in range(WF):
            needed = lax.rem(my_start + shift + j, windows)
            next_at[j] = owner_ref[needed] * capacity + j // windows

    for which, (ref, now, sem, gain) in enumerate(
        ((q_ref, q_now, q_load, qg_ref), (k_ref, k_now, k_load, kg_ref))
    ):

        def norm_block(t, carry, which=which, ref=ref, now=now, sem=sem, gain=gain):
            blocks = chunk // ROWS

            @pl.when(lax.rem(t, blocks) == 0)
            def _():
                load(ref, now, sem, t // blocks).wait()

            rows = pl.ds(pl.multiple_of(t * ROWS, ROWS), ROWS)
            floats = now[rows, :].astype(jnp.float32)
            mean_square = jnp.mean(floats * floats, axis=-1, keepdims=True)
            scaled = (floats * lax.rsqrt(mean_square + 1e-06) * gain[...]).astype(jnp.bfloat16)
            for u in range(ulysses):
                for s in range(steps):
                    at = (u * steps + s) * head
                    stage[which, u, s, rows, :] = scaled[:, at : at + head]
            return carry

        lax.fori_loop(0, tokens // ROWS, norm_block, 0)
        for s in range(AHEAD):
            send_scored(which, s)

    tables()

    scale = 1.0 / math.sqrt(head)

    def attention(s):
        arrived(inbox.at[0, s], q_recv.at[s])
        arrived(inbox.at[1, s], k_recv.at[s])
        arrived(vbox.at[s], v_recv.at[s])

        @pl.when(s + AHEAD < steps)
        def _():
            send_scored(0, s + AHEAD)
            send_scored(1, s + AHEAD)

        @pl.when(s + VALUES_AHEAD < steps)
        def _():
            send_values(s + VALUES_AHEAD)

        keys = inbox[1, s].reshape(ulysses * tokens, head)
        values = vbox[s].reshape(ulysses * tokens, head)
        for u in range(ulysses):
            scores = (
                lax.dot_general(
                    inbox[0, s, u],
                    keys,
                    (((1,), (1,)), ((), ())),
                    preferred_element_type=jnp.float32,
                )
                * scale
            )
            exponent = jnp.exp(scores - jnp.max(scores, axis=-1, keepdims=True))
            inverse_sum = 1.0 / jnp.sum(exponent, axis=-1, keepdims=True)
            weights = (exponent * inverse_sum).astype(jnp.bfloat16)
            result = jnp.dot(weights, values, preferred_element_type=jnp.float32)
            attended[:, u] = result.astype(jnp.bfloat16).reshape(WF, local, head)
        for o in range(windows):
            for c in range(capacity):
                z_out[s, o, c] = attended[send_pos[o * capacity + c]]
        spread(
            lambda o: z_out.at[s, o],
            lambda o: z_in.at[s, pl.ds(o * capacity, capacity)],
            zo_send.at[s],
            zo_recv.at[s],
            "win",
        )

    def blend(s):
        arrived(z_in.at[s], zo_recv.at[s])
        z_now[...] = z_in[s]
        for f in range(FR):
            numerator = first_w[f] * z_now[first_at[f]].astype(jnp.float32)
            numerator += second_w[f] * z_now[second_at[f]].astype(jnp.float32)
            x_out[s, :, f] = (numerator / (first_w[f] + second_w[f])).astype(jnp.bfloat16)
        spread(
            lambda u: x_out.at[s, u],
            lambda u: x_in.at[s, u],
            xo_send.at[s],
            xo_recv.at[s],
            "uly",
        )

    def give_back(s):
        arrived(x_in.at[s], xo_recv.at[s])
        x_now[...] = x_in[s]
        for o in range(windows):
            for c in range(capacity):
                r_out[s, o, c] = x_now[:, target_slot[o * capacity + c]]
        spread(
            lambda o: r_out.at[s, o],
            lambda o: r_in.at[s, pl.ds(o * capacity, capacity)],
            ro_send.at[s],
            ro_recv.at[s],
            "win",
        )
        for u in range(ulysses):
            pltpu.make_async_copy(
                x_in.at[s, u], owned_ref.at[:, :, columns(u, s)], own_sem.at[s]
            ).start()

    def finish(s):
        arrived(r_in.at[s], ro_recv.at[s])
        z_now[...] = r_in[s]
        for j in range(WF):
            next_out[s, :, j] = z_now[next_at[j]]
        for u in range(ulysses):
            pltpu.make_async_copy(
                next_out.at[s, u], next_ref.at[:, :, columns(u, s)], next_sem.at[s]
            ).start()

    def step(i, carry):
        for lag, work in (
            (0, attention),
            (LAG_BLEND, blend),
            (LAG_RETURN, give_back),
            (LAG_LAST, finish),
        ):

            @pl.when((i >= lag) & (i < steps + lag))
            def _(lag=lag, work=work):
                work(i - lag)

        return carry

    lax.fori_loop(0, steps + LAG_LAST, step, 0)

    def sent(s, carry):
        arrived(inbox.at[0, s, pl.ds(0, ulysses - 1)], q_send.at[s])
        arrived(inbox.at[1, s, pl.ds(0, ulysses - 1)], k_send.at[s])
        arrived(vbox.at[s, pl.ds(0, ulysses - 1)], v_send.at[s])
        arrived(z_out.at[s, pl.ds(0, windows - 1)], zo_send.at[s])
        arrived(x_out.at[s, pl.ds(0, ulysses - 1)], xo_send.at[s])
        arrived(r_out.at[s, pl.ds(0, windows - 1)], ro_send.at[s])
        arrived(x_in.at[s], own_sem.at[s])
        arrived(next_out.at[s], next_sem.at[s])
        return carry

    lax.fori_loop(0, steps, sent, 0)


def per_device(
    query_rows,
    key_rows,
    value_rows,
    query_gain,
    key_gain,
    window_start,
    owner_of_phase,
    blend_weight,
):
    windows = lax.axis_size("win")
    ulysses = lax.axis_size("uly")
    capacity = (WF + windows - 1) // windows
    local = query_rows.shape[2]
    features = query_rows.shape[3]
    head = features // HEADS
    steps = HEADS // ulysses
    tokens = WF * local
    smem = pl.BlockSpec(memory_space=pltpu.SMEM)
    vmem = pl.BlockSpec(memory_space=pltpu.VMEM)
    hbm = pl.BlockSpec(memory_space=pl.ANY)
    bf16 = jnp.bfloat16
    sems = pltpu.SemaphoreType.DMA((steps,))
    frame = (ulysses, local, head)
    owned, next_rows = pl.pallas_call(
        functools.partial(fused, (ulysses, windows, capacity, steps, head, tokens)),
        out_shape=(
            jax.ShapeDtypeStruct((FR, local, features), bf16),
            jax.ShapeDtypeStruct((WF, local, features), bf16),
        ),
        in_specs=[smem] * 3 + [hbm] * 3 + [vmem] * 2,
        out_specs=(hbm, hbm),
        scratch_shapes=[
            pltpu.VMEM((tokens, features), bf16),
            pltpu.VMEM((tokens, features), bf16),
            pltpu.VMEM((steps, ulysses, WF, local, head), bf16),
            pltpu.VMEM((2, ulysses, steps, tokens, head), bf16),
            pltpu.VMEM((2, steps, ulysses, tokens, head), bf16),
            pltpu.VMEM((steps, ulysses, tokens, head), bf16),
            pltpu.VMEM((WF,) + frame, bf16),
            pltpu.VMEM((steps, windows, capacity) + frame, bf16),
            pltpu.VMEM((steps, windows * capacity) + frame, bf16),
            pltpu.VMEM((steps, ulysses, FR, local, head), bf16),
            pltpu.VMEM((steps, ulysses, FR, local, head), bf16),
            pltpu.VMEM((steps, windows, capacity) + frame, bf16),
            pltpu.VMEM((steps, windows * capacity) + frame, bf16),
            pltpu.VMEM((windows * capacity,) + frame, bf16),
            pltpu.VMEM((ulysses, FR, local, head), bf16),
            pltpu.SMEM((windows,), jnp.int32),
            pltpu.SMEM((windows * capacity,), jnp.int32),
            pltpu.SMEM((FR,), jnp.int32),
            pltpu.SMEM((FR,), jnp.int32),
            pltpu.SMEM((FR,), jnp.float32),
            pltpu.SMEM((FR,), jnp.float32),
            pltpu.SMEM((windows * capacity,), jnp.int32),
            pltpu.SMEM((WF,), jnp.int32),
        ]
        + [sems] * 14
        + [pltpu.SemaphoreType.DMA((CHUNKS,))] * 2,
        compiler_params=pltpu.CompilerParams(
            collective_id=0, has_side_effects=True, vmem_limit_bytes=66 * 1000 * 1000
        ),
    )(
        window_start,
        owner_of_phase,
        blend_weight,
        query_rows.reshape(tokens, features),
        key_rows.reshape(tokens, features),
        value_rows.reshape(tokens, features),
        query_gain.reshape(1, features),
        key_gain.reshape(1, features),
    )
    return (owned, next_rows[None])


def solution(mesh):
    placed = (
        P(("grp", "win"), None, "uly", None),
        P(("grp", "win"), None, "uly", None),
        P(("grp", "win"), None, "uly", None),
        P(),
        P(),
        P("grp"),
        P("grp"),
        P("grp", None),
    )
    return jax.shard_map(
        per_device,
        mesh=mesh,
        in_specs=placed,
        out_specs=(P(("grp", "win"), "uly", None), P(("grp", "win"), None, "uly", None)),
        check_vma=False,
    )
```

```python
import functools
import math

import jax
import jax.numpy as jnp
from jax import lax
from jax.experimental import pallas as pl
from jax.experimental.pallas import tpu as pltpu
from jax.sharding import PartitionSpec as P

HEADS = 40
WF = 16
FR = 12
VALUES_AHEAD = 2
CHUNKS = 4
LAG_BLEND = 1
LAG_RETURN = 2
LAG_LAST = 3
ROWS = 16


def fused(
    dims,
    start_ref,
    owner_ref,
    weight_ref,
    q_ref,
    k_ref,
    v_ref,
    qg_ref,
    kg_ref,
    owned_ref,
    next_ref,
    q_now,
    k_now,
    next_out,
    root,
    stage,
    inbox,
    vbox,
    attended,
    z_out,
    z_in,
    x_out,
    x_in,
    r_out,
    r_in,
    z_now,
    x_now,
    inverse,
    send_pos,
    first_at,
    second_at,
    first_w,
    second_w,
    target_slot,
    next_at,
    q_send,
    q_recv,
    k_send,
    k_recv,
    v_send,
    v_recv,
    zo_send,
    zo_recv,
    xo_send,
    xo_recv,
    ro_send,
    ro_recv,
    own_sem,
    next_sem,
    q_load,
    k_load,
):
    ulysses, windows, capacity, steps, head, tokens = dims
    local = tokens // WF
    me = lax.axis_index("uly")
    my_window = lax.axis_index("win")

    def peer(d):
        return lax.rem(me + d, ulysses)

    def far(d):
        return lax.rem(my_window + d, windows)

    chunk = tokens // CHUNKS

    def load(ref, now, sem, c):
        rows = pl.ds(pl.multiple_of(c * chunk, chunk), chunk)
        return pltpu.make_async_copy(ref.at[rows], now.at[rows], sem.at[c])

    for ref, now, sem in ((q_ref, q_now, q_load), (k_ref, k_now, k_load)):
        for c in range(CHUNKS):
            load(ref, now, sem, c).start()

    barrier = pltpu.get_barrier_semaphore()
    for d in range(1, ulysses):
        pl.semaphore_signal(
            barrier, inc=1, device_id={"uly": peer(d)}, device_id_type=pl.DeviceIdType.MESH
        )
    for d in range(1, windows):
        pl.semaphore_signal(
            barrier, inc=1, device_id={"win": far(d)}, device_id_type=pl.DeviceIdType.MESH
        )
    pl.semaphore_wait(barrier, ulysses + windows - 2)

    def spread(source, target, send, recv, axis):
        mine = me if axis == "uly" else my_window
        count = ulysses if axis == "uly" else windows
        for d in range(1, count):
            to = lax.rem(mine + d, count)
            pltpu.make_async_remote_copy(
                src_ref=source(to),
                dst_ref=target(mine),
                send_sem=send,
                recv_sem=recv,
                device_id={axis: to},
                device_id_type=pl.DeviceIdType.MESH,
            ).start()
        pltpu.make_async_copy(source(mine), target(mine), recv).start()

    def arrived(ref, sem):
        pltpu.make_async_copy(ref, ref, sem).wait()

    def columns(u, s):
        return pl.ds(pl.multiple_of((u * steps + s) * head, head), head)

    def scale_columns(which, s):
        now, gain = ((q_now, qg_ref), (k_now, kg_ref))[which]
        for u in range(ulysses):
            at = columns(u, s)
            scaled = now[:, at].astype(jnp.float32) * root[which] * gain[:, at]
            stage[which, u, s] = scaled.astype(jnp.bfloat16)

    def send_values(s):
        spread(
            lambda u: v_ref.at[:, columns(u, s)],
            lambda u: vbox.at[s, u],
            v_send.at[s],
            v_recv.at[s],
            "uly",
        )

    def send_scored(which, s):
        spread(
            lambda u: stage.at[which, u, s],
            lambda u: inbox.at[which, s, u],
            (q_send, k_send)[which].at[s],
            (q_recv, k_recv)[which].at[s],
            "uly",
        )

    for s in range(VALUES_AHEAD):
        send_values(s)

    frames_total = FR * windows
    shift = FR // 2

    def tables():
        my_start = start_ref[my_window]

        def invert(o, carry):
            def seek(phase, found):
                return jnp.where(owner_ref[phase] == o, phase, found)

            inverse[o] = lax.fori_loop(0, windows, seek, jnp.int32(0))
            return carry

        lax.fori_loop(0, windows, invert, 0)
        my_phase = inverse[my_window]

        def per_window(o, carry):
            for c in range(capacity):
                ahead = lax.rem(inverse[o] - my_start + frames_total, windows) + c * windows
                send_pos[o * capacity + c] = jnp.minimum(ahead, WF - 1)
                base = start_ref[o] + shift
                wanted = lax.rem(my_phase - base + 2 * frames_total, windows) + c * windows
                target_slot[o * capacity + c] = lax.rem(base + wanted, frames_total) // windows
            return carry

        lax.fori_loop(0, windows, per_window, 0)

        for f in range(FR):
            frame = f * windows + my_phase
            home = frame // FR
            before = lax.rem(home + windows - 1, windows)
            weight, place = [], []
            for w in (home, before):
                offset = lax.rem(frame - start_ref[w] + frames_total, frames_total)
                held = jnp.minimum(offset, WF - 1)
                weight.append(jnp.where(offset < WF, weight_ref[w, held], 0).astype(jnp.float32))
                place.append(w * capacity + held // windows)
            first_w[f], second_w[f] = weight
            first_at[f], second_at[f] = place
        for j in range(WF):
            needed = lax.rem(my_start + shift + j, windows)
            next_at[j] = owner_ref[needed] * capacity + j // windows

    for which, (ref, now, sem, gain) in enumerate(
        ((q_ref, q_now, q_load, qg_ref), (k_ref, k_now, k_load, kg_ref))
    ):

        def norm_block(t, carry, which=which, ref=ref, now=now, sem=sem, gain=gain):
            blocks = chunk // ROWS

            @pl.when(lax.rem(t, blocks) == 0)
            def _():
                load(ref, now, sem, t // blocks).wait()

            rows = pl.ds(pl.multiple_of(t * ROWS, ROWS), ROWS)
            floats = now[rows, :].astype(jnp.float32)
            mean_square = jnp.mean(floats * floats, axis=-1, keepdims=True)
            root[which, rows, :] = jnp.broadcast_to(
                lax.rsqrt(mean_square + 1e-06), (ROWS, head)
            )
            return carry

        lax.fori_loop(0, tokens // ROWS, norm_block, 0)
        scale_columns(which, 0)

    send_scored(0, 0)
    send_scored(1, 0)
    for which in range(2):
        scale_columns(which, 1)

    tables()

    scale = 1.0 / math.sqrt(head)

    def attention(s):
        arrived(inbox.at[0, s], q_recv.at[s])
        arrived(inbox.at[1, s], k_recv.at[s])
        arrived(vbox.at[s], v_recv.at[s])

        @pl.when(s + 1 < steps)
        def _():
            send_scored(0, s + 1)
            send_scored(1, s + 1)

        @pl.when(s + VALUES_AHEAD < steps)
        def _():
            send_values(s + VALUES_AHEAD)

        keys = inbox[1, s].reshape(ulysses * tokens, head)
        values = vbox[s].reshape(ulysses * tokens, head)
        for u in range(ulysses):
            scores = (
                lax.dot_general(
                    inbox[0, s, u],
                    keys,
                    (((1,), (1,)), ((), ())),
                    preferred_element_type=jnp.float32,
                )
                * scale
            )
            exponent = jnp.exp(scores - jnp.max(scores, axis=-1, keepdims=True))
            inverse_sum = 1.0 / jnp.sum(exponent, axis=-1, keepdims=True)
            weights = (exponent * inverse_sum).astype(jnp.bfloat16)
            result = jnp.dot(weights, values, preferred_element_type=jnp.float32)
            attended[:, u] = result.astype(jnp.bfloat16).reshape(WF, local, head)
        for o in range(windows):
            for c in range(capacity):
                z_out[s, o, c] = attended[send_pos[o * capacity + c]]
        spread(
            lambda o: z_out.at[s, o],
            lambda o: z_in.at[s, pl.ds(o * capacity, capacity)],
            zo_send.at[s],
            zo_recv.at[s],
            "win",
        )

        @pl.when(s + 2 < steps)
        def _():
            for which in range(2):
                scale_columns(which, s + 2)

    def blend(s):
        arrived(z_in.at[s], zo_recv.at[s])
        z_now[...] = z_in[s]
        for f in range(FR):
            numerator = first_w[f] * z_now[first_at[f]].astype(jnp.float32)
            numerator += second_w[f] * z_now[second_at[f]].astype(jnp.float32)
            x_out[s, :, f] = (numerator / (first_w[f] + second_w[f])).astype(jnp.bfloat16)
        spread(
            lambda u: x_out.at[s, u],
            lambda u: x_in.at[s, u],
            xo_send.at[s],
            xo_recv.at[s],
            "uly",
        )

    def give_back(s):
        arrived(x_in.at[s], xo_recv.at[s])
        x_now[...] = x_in[s]
        for o in range(windows):
            for c in range(capacity):
                r_out[s, o, c] = x_now[:, target_slot[o * capacity + c]]
        spread(
            lambda o: r_out.at[s, o],
            lambda o: r_in.at[s, pl.ds(o * capacity, capacity)],
            ro_send.at[s],
            ro_recv.at[s],
            "win",
        )
        for u in range(ulysses):
            pltpu.make_async_copy(
                x_in.at[s, u], owned_ref.at[:, :, columns(u, s)], own_sem.at[s]
            ).start()

    def finish(s):
        arrived(r_in.at[s], ro_recv.at[s])
        z_now[...] = r_in[s]
        for j in range(WF):
            next_out[s, :, j] = z_now[next_at[j]]
        for u in range(ulysses):
            pltpu.make_async_copy(
                next_out.at[s, u], next_ref.at[:, :, columns(u, s)], next_sem.at[s]
            ).start()

    def step(i, carry):
        for lag, work in (
            (0, attention),
            (LAG_RETURN, give_back),
            (LAG_BLEND, blend),
            (LAG_LAST, finish),
        ):

            @pl.when((i >= lag) & (i < steps + lag))
            def _(lag=lag, work=work):
                work(i - lag)

        return carry

    lax.fori_loop(0, steps + LAG_LAST, step, 0)

    def sent(s, carry):
        arrived(inbox.at[0, s, pl.ds(0, ulysses - 1)], q_send.at[s])
        arrived(inbox.at[1, s, pl.ds(0, ulysses - 1)], k_send.at[s])
        arrived(vbox.at[s, pl.ds(0, ulysses - 1)], v_send.at[s])
        arrived(z_out.at[s, pl.ds(0, windows - 1)], zo_send.at[s])
        arrived(x_out.at[s, pl.ds(0, ulysses - 1)], xo_send.at[s])
        arrived(r_out.at[s, pl.ds(0, windows - 1)], ro_send.at[s])
        arrived(x_in.at[s], own_sem.at[s])
        arrived(next_out.at[s], next_sem.at[s])
        return carry

    lax.fori_loop(0, steps, sent, 0)


def per_device(
    query_rows,
    key_rows,
    value_rows,
    query_gain,
    key_gain,
    window_start,
    owner_of_phase,
    blend_weight,
):
    windows = lax.axis_size("win")
    ulysses = lax.axis_size("uly")
    capacity = (WF + windows - 1) // windows
    local = query_rows.shape[2]
    features = query_rows.shape[3]
    head = features // HEADS
    steps = HEADS // ulysses
    tokens = WF * local
    smem = pl.BlockSpec(memory_space=pltpu.SMEM)
    vmem = pl.BlockSpec(memory_space=pltpu.VMEM)
    hbm = pl.BlockSpec(memory_space=pl.ANY)
    bf16 = jnp.bfloat16
    sems = pltpu.SemaphoreType.DMA((steps,))
    frame = (ulysses, local, head)
    owned, next_rows = pl.pallas_call(
        functools.partial(fused, (ulysses, windows, capacity, steps, head, tokens)),
        out_shape=(
            jax.ShapeDtypeStruct((FR, local, features), bf16),
            jax.ShapeDtypeStruct((WF, local, features), bf16),
        ),
        in_specs=[smem] * 3 + [hbm] * 3 + [vmem] * 2,
        out_specs=(hbm, hbm),
        scratch_shapes=[
            pltpu.VMEM((tokens, features), bf16),
            pltpu.VMEM((tokens, features), bf16),
            pltpu.VMEM((steps, ulysses, WF, local, head), bf16),
            pltpu.VMEM((2, tokens, head), jnp.float32),
            pltpu.VMEM((2, ulysses, steps, tokens, head), bf16),
            pltpu.VMEM((2, steps, ulysses, tokens, head), bf16),
            pltpu.VMEM((steps, ulysses, tokens, head), bf16),
            pltpu.VMEM((WF,) + frame, bf16),
            pltpu.VMEM((steps, windows, capacity) + frame, bf16),
            pltpu.VMEM((steps, windows * capacity) + frame, bf16),
            pltpu.VMEM((steps, ulysses, FR, local, head), bf16),
            pltpu.VMEM((steps, ulysses, FR, local, head), bf16),
            pltpu.VMEM((steps, windows, capacity) + frame, bf16),
            pltpu.VMEM((steps, windows * capacity) + frame, bf16),
            pltpu.VMEM((windows * capacity,) + frame, bf16),
            pltpu.VMEM((ulysses, FR, local, head), bf16),
            pltpu.SMEM((windows,), jnp.int32),
            pltpu.SMEM((windows * capacity,), jnp.int32),
            pltpu.SMEM((FR,), jnp.int32),
            pltpu.SMEM((FR,), jnp.int32),
            pltpu.SMEM((FR,), jnp.float32),
            pltpu.SMEM((FR,), jnp.float32),
            pltpu.SMEM((windows * capacity,), jnp.int32),
            pltpu.SMEM((WF,), jnp.int32),
        ]
        + [sems] * 14
        + [pltpu.SemaphoreType.DMA((CHUNKS,))] * 2,
        compiler_params=pltpu.CompilerParams(
            collective_id=0, has_side_effects=True, vmem_limit_bytes=66 * 1000 * 1000
        ),
    )(
        window_start,
        owner_of_phase,
        blend_weight,
        query_rows.reshape(tokens, features),
        key_rows.reshape(tokens, features),
        value_rows.reshape(tokens, features),
        query_gain.reshape(1, features),
        key_gain.reshape(1, features),
    )
    return (owned, next_rows[None])


def solution(mesh):
    placed = (
        P(("grp", "win"), None, "uly", None),
        P(("grp", "win"), None, "uly", None),
        P(("grp", "win"), None, "uly", None),
        P(),
        P(),
        P("grp"),
        P("grp"),
        P("grp", None),
    )
    return jax.shard_map(
        per_device,
        mesh=mesh,
        in_specs=placed,
        out_specs=(P(("grp", "win"), "uly", None), P(("grp", "win"), None, "uly", None)),
        check_vma=False,
    )
```
